32 devices in a mesh: ctx: 16 (over z, y, core), head: 2 (over x).
Axes of the slice: x: 2, y: 2, z: 4, core: 2. Of those that a mesh axis runs over, the one named last changes fastest.
Arguments:
- query_gate: bfloat16 [4096, 4096], P(('ctx', 'head')), may hold values from -6 to 6
- key_gate: bfloat16 [4096, 4096], P(('ctx', 'head')), may hold values from -6 to 6
- values: bfloat16 [4096, 4096], P(('ctx', 'head')), may hold values from -6 to 6
- rate_mix: float32 [512, 8], replicated, may hold values from 0 to 1
- residue: float32 [512, 8], replicated, may hold values from -4.5 to 4.5
- skip_gain: float32 [4096], replicated, may hold values from 0.25 to 1.75
- doc_lengths: int32 [16], replicated, may hold values from 1 to 1024, 4096 in all
Outputs:
- gated_out: bfloat16 [4096, 4096], P(('ctx', 'head'))
The draws below stay inside these ranges and needn't reach their ends.
Inputs may be any that keep to these rules, and one draw needn't show every extreme that they name: `doc_lengths`: the lengths sum to 4096, and the longest is exactly 1024.
All inputs are finite; a program needn't handle non-finite values.
Results may differ from the reference program's by a relative error of at most 0.014.
Values may be sent and summed in bfloat16 or wider, within the bound.
A program may use at most 64 MiB of HBM per device.

```python
import math
import jax
import jax.numpy as jnp
import numpy as np
from jax import lax

C = 4096
G = 512
MODES = 8
NDOC = 16
SEQ = 4096


def draw_rate_mix(key, part):
    first_key = jax.random.fold_in(key, 0)
    uniform_part = jax.random.uniform(first_key, (G, MODES), jnp.float32)
    return uniform_part ** 0.7


def shard_levels(stream_key, dims, pieces, low, top_value):
    level = 1.0
    for dim, parts in pieces:
        steps = jax.random.uniform(jax.random.fold_in(jax.random.fold_in(stream_key, 6), dim), (parts,), jnp.float32, low / len(pieces), top_value / len(pieces))
        level = level * jnp.repeat(jnp.exp(steps), dims[dim] // parts).reshape((-1,) + (1,) * (len(dims) - 1 - dim))
    return level


def profile(number_of, total, limit, slope):
    loads = [(1 << 20) // math.isqrt(standing ** slope) + 1 for standing in range(2, number_of + 1)]
    rest, counts = total - limit - (number_of - 1), [1] * (number_of - 1)
    while rest > 0:
        candidates = [i for i in range(number_of - 1) if counts[i] < limit]
        pool, budget = sum([loads[i] for i in candidates]), rest
        for i in candidates:
            extra = min(limit - counts[i], max(1, budget * loads[i] // pool), rest)
            counts[i] = counts[i] + extra
            rest = rest - extra
    return np.array([limit] + counts)


def uneven(key, amount, total, reach, slope):
    if amount == 2:
        one = jax.random.randint(key, (), max(1, total - reach), min(reach, total - 1) + 1)
        return jnp.stack([one, total - one])
    sizes = jnp.asarray(profile(amount, total, reach, slope), jnp.int32)
    couples = (amount - 1) // 2
    donor, sink = sizes[1:1 + 2 * couples:2], sizes[2:2 + 2 * couples:2]
    room = jnp.minimum(donor - 1, reach - sink)
    moved = jax.random.randint(jax.random.fold_in(key, 1), (couples,), 0, 1 << 20) % (room + 1)
    sizes = sizes.at[1:1 + 2 * couples:2].set(donor - moved).at[2:2 + 2 * couples:2].set(sink + moved)
    return sizes[jax.random.permutation(jax.random.fold_in(key, 2), amount)]


def normal_values(stream_key, dims, spread, bound, pieces=(), kind=jnp.bfloat16):
    loudness = shard_levels(stream_key, dims, pieces, -0.22, 0.18) if pieces else 1.0
    result = jax.random.normal(stream_key, dims, jnp.float32) * spread * loudness
    return jnp.minimum(jnp.maximum(result, -bound), bound).astype(kind)


def setup_inputs(seed: int = 0) -> dict:
    streams_of = jax.random.split(jax.random.key(seed), 8)
    return {
        "query_gate": normal_values(streams_of[0], (SEQ, C), 1.0, 6.0, ((0, 32),)),
        "key_gate": normal_values(streams_of[1], (SEQ, C), 1.0, 6.0, ((0, 32),)),
        "values": normal_values(streams_of[2], (SEQ, C), 1.0, 6.0, ((0, 32),)),
        "rate_mix": draw_rate_mix(jax.random.fold_in(streams_of[7], 71), 0),
        "residue": normal_values(streams_of[4], (G, MODES), 0.75, 4.5, (), jnp.float32),
        "skip_gain": jnp.clip(1.0 + 0.15 * jax.random.normal(streams_of[5], (C,), jnp.float32), 0.25, 1.75),
        "doc_lengths": uneven(streams_of[6], NDOC, SEQ, SEQ // 4, 2).astype(jnp.int32),
    }


tile_rows = 128
highest = lax.Precision.HIGHEST

def doc_index(positions, doc_lengths):
    doc_ends = jnp.cumsum(doc_lengths).astype(jnp.int32)
    hits = (positions[:, None] >= doc_ends[None, :]).astype(jnp.int32)
    return lax.optimization_barrier(jnp.sum(hits, axis=1)).astype(jnp.int32)

def mode_tables(rate_mix, residue, total_tokens):
    decay_rate = jnp.exp(-math.log(30.0) - rate_mix * math.log(float(total_tokens)))
    weights = residue * jnp.sqrt(-jnp.expm1(-2.0 * decay_rate))
    return (decay_rate, weights)

def tile_conv(mixed_tile, doc_ids, doc_prev, decay_rate, weights, carried):
    row_count = mixed_tile.shape[0]
    groups, mode_count = decay_rate.shape
    group_width = mixed_tile.shape[1] // groups
    offsets = jnp.arange(row_count).astype(decay_rate.dtype)
    rising = jnp.exp(-decay_rate[:, :, None] * offsets[None, None, :])
    falling = jnp.exp(decay_rate[:, :, None] * offsets[None, None, :])
    left_side = weights[:, :, None] * rising
    kernel = jnp.einsum('gri,grj->gij', left_side, falling, precision=highest)
    allowed = (doc_ids[:, None] == doc_ids[None, :]) & (offsets[:, None] >= offsets[None, :])
    kernel = jnp.where(allowed[None], kernel, 0.0)
    mixed_float = mixed_tile.astype(decay_rate.dtype).reshape(row_count, groups, group_width)
    inner_term = jnp.einsum('gij,jgc->igc', kernel, mixed_float, precision=highest)
    entering = left_side * jnp.exp(-decay_rate)[:, :, None]
    cross_term = jnp.einsum('gri,rgc->igc', entering, carried.reshape(mode_count, groups, group_width), precision=highest)
    linked = (doc_ids == doc_prev).astype(decay_rate.dtype)
    total_term = inner_term + cross_term * linked[:, None, None]
    return total_term.reshape(row_count, groups * group_width)

def tile_state(mixed_tile, doc_ids, doc_prev, decay_rate):
    row_count = mixed_tile.shape[0]
    groups, mode_count = decay_rate.shape
    group_width = mixed_tile.shape[1] // groups
    offsets = jnp.arange(row_count).astype(decay_rate.dtype)
    tail_mask = (doc_ids == doc_ids[row_count - 1]).astype(decay_rate.dtype)
    tail_decay = jnp.exp(-decay_rate[:, :, None] * (row_count - 1 - offsets)[None, None, :]) * tail_mask[None, None, :]
    mixed_float = mixed_tile.astype(decay_rate.dtype).reshape(row_count, groups, group_width)
    local_state = jnp.einsum('grj,jgc->rgc', tail_decay, mixed_float, precision=highest)
    keep_flag = (doc_ids[row_count - 1] == doc_prev).astype(decay_rate.dtype)
    return (local_state.reshape(mode_count, groups * group_width), keep_flag)

def reference(query_gate, key_gate, values, rate_mix, residue, skip_gain, doc_lengths):
    decay_rate, weights = mode_tables(rate_mix, residue, SEQ)
    group_width = C // G
    decay_full = jnp.repeat(decay_rate.T, group_width, axis=1)
    mixed = key_gate * values
    tile_count = SEQ // tile_rows

    def advance(carried, tile_index):
        tile_start = tile_index * tile_rows
        mixed_tile = lax.dynamic_slice_in_dim(mixed, tile_start, tile_rows, 0)
        positions = (tile_start + jnp.arange(tile_rows)).astype(jnp.int32)
        doc_ids = doc_index(positions, doc_lengths)
        before = jnp.maximum(tile_start - 1, 0).astype(jnp.int32).reshape(1)
        doc_prev = doc_index(before, doc_lengths)[0]
        convolved = tile_conv(mixed_tile, doc_ids, doc_prev, decay_rate, weights, carried)
        convolved = convolved + skip_gain[None, :] * mixed_tile.astype(decay_rate.dtype)
        local_state, keep_flag = tile_state(mixed_tile, doc_ids, doc_prev, decay_rate)
        carried = keep_flag * jnp.exp(-decay_full * tile_rows) * carried + local_state
        return (carried, convolved.astype(jnp.bfloat16))
    start_state = jnp.zeros((MODES, C), dtype=decay_rate.dtype)
    _, smoothed = lax.scan(advance, start_state, jnp.arange(tile_count).astype(jnp.int32))
    smoothed = smoothed.reshape(SEQ, C)
    return query_gate * smoothed
```

```python
import functools
import math

import jax
import jax.numpy as jnp
from jax import lax
from jax.experimental import pallas as pl
from jax.experimental.pallas import tpu as pltpu
from jax.sharding import PartitionSpec as P

LANES = 128
MESH = pl.DeviceIdType.MESH
f32 = jnp.float32
bf16 = jnp.bfloat16


def doc_start(tokens, ends):
    start = jnp.zeros_like(tokens)
    for end in ends:
        start = jnp.maximum(start, jnp.where(tokens >= end, end, 0))
    return start


def kernel(cfg, lengths, q_hbm, k_hbm, v_hbm, rate_rows, weight_rows, chan_rate, chan_weight, skip,
           out_hbm, q_buf, k_buf, v_buf, out_buf, mixed, inner, cross_table,
           state_buf, gather_buf, prefix_buf, reply_buf, enter_buf, exit_buf, far_buf,
           load_sem, store_sem, send1, recv1, send2, recv2, send3, recv3):
    ctx_count, head_count, block, reach = cfg
    devices = ctx_count * head_count
    tok, chans = mixed.shape
    modes = chan_rate.shape[0]
    lane_blocks = chans // LANES
    per_slice = lane_blocks // block
    group_width = LANES * modes // LANES
    block_count = devices // block
    me = lax.axis_index("ctx") * head_count + lax.axis_index("head")
    zone, pos = me // block, me % block
    span = me * tok

    def where_is(index):
        return (index // head_count, index % head_count)

    loads = []
    for n, (src, dst) in enumerate(((k_hbm, k_buf), (v_hbm, v_buf), (q_hbm, q_buf))):
        loads.append(pltpu.make_async_copy(src, dst, load_sem.at[n]))
        loads[-1].start()

    barrier = pltpu.get_barrier_semaphore()
    mates = [zone * block + (pos + s) % block for s in range(1, block)]
    for mate in mates:
        pl.semaphore_signal(barrier, inc=1, device_id=where_is(mate), device_id_type=MESH)
    for k in range(1, reach + 1):
        @pl.when(zone + k < block_count)
        def _(k=k):
            pl.semaphore_signal(barrier, inc=1, device_id=where_is(me + k * block), device_id_type=MESH)

        @pl.when(zone >= k)
        def _(k=k):
            pl.semaphore_signal(barrier, inc=1, device_id=where_is(me - k * block), device_id_type=MESH)

    ends, total = [], jnp.int32(0)
    for n in range(lengths.shape[0]):
        total = total + lengths[n]
        ends.append(total)

    def start_of(token):
        return doc_start(jnp.full((1, LANES), token, jnp.int32), ends)

    rows = lax.broadcasted_iota(jnp.int32, (tok, LANES), 0)
    gr = lax.broadcasted_iota(jnp.int32, (LANES, LANES), 0) // modes
    gc = lax.broadcasted_iota(jnp.int32, (LANES, LANES), 1) // group_width
    diagonal = gr == gc

    tail_start = start_of(span + tok - 1) - span
    tail = rows >= tail_start
    left = (tok - 1 - rows).astype(f32)

    loads[0].wait()
    loads[1].wait()

    def local(b, _):
        cols = pl.ds(pl.multiple_of(b * LANES, LANES), LANES)
        x = k_buf[:, cols] * v_buf[:, cols]
        mixed[:, cols] = x
        rate = rate_rows[pl.ds(b, 1), :]
        table = jnp.where(tail, jnp.exp(-rate * left), 0.0).astype(bf16)
        full = lax.dot_general(table, x, (((0,), (0,)), ((), ())), preferred_element_type=f32)
        full = jnp.where(diagonal, full, 0.0)
        state = jnp.sum(full.reshape(LANES // modes, modes, LANES), axis=0)
        state_buf[b // per_slice, :, pl.ds(pl.multiple_of((b % per_slice) * LANES, LANES), LANES)] = state.astype(state_buf.dtype)
        return 0

    lax.fori_loop(0, lane_blocks, local, 0, unroll=4)

    expected = (block - 1)
    for k in range(1, reach + 1):
        expected = expected + jnp.where(zone + k < block_count, 1, 0) + jnp.where(zone >= k, 1, 0)
    pl.semaphore_wait(barrier, expected)

    first = []
    for s, mate in enumerate(mates):
        first.append(pltpu.make_async_remote_copy(
            src_ref=state_buf.at[(pos + s + 1) % block], dst_ref=gather_buf.at[pos],
            send_sem=send1.at[s], recv_sem=recv1.at[s],
            device_id=where_is(mate), device_id_type=MESH))
        first[-1].start()
    gather_buf[pos] = state_buf[pos]

    row_tok = span + rows
    row_start = doc_start(row_tok, ends) - span
    lane_iota = lax.broadcasted_iota(jnp.int32, (tok, tok), 1)
    row_iota = lax.broadcasted_iota(jnp.int32, (tok, tok), 0)
    mask = jnp.where((lane_iota >= row_start[:, :1]) & (lane_iota <= row_iota), 1.0, 0.0).astype(bf16)
    linked = row_start < 0
    ahead = (rows + 1).astype(f32)

    wide = 2 * LANES
    wide_blocks = chans // wide
    eights = lax.broadcasted_iota(jnp.int32, (8, wide), 0).astype(f32)

    def conv(b, _):
        cols = pl.ds(pl.multiple_of(b * wide, wide), wide)
        x = mixed[:, cols].astype(f32)
        total = skip[:, cols] * x
        for r in range(modes):
            rate = chan_rate[r:r + 1, cols]
            up = jnp.exp(rate * eights)
            down = chan_weight[r:r + 1, cols] * jnp.exp(-rate * eights)
            up_step = jnp.broadcast_to(jnp.exp(8.0 * rate), up.shape)
            down_step = jnp.broadcast_to(jnp.exp(-8.0 * rate), up.shape)
            ups, downs = [], []
            for _p in range(tok // 8):
                ups.append(up)
                downs.append(down)
                up, down = up * up_step, down * down_step
            scaled = (x * jnp.concatenate(ups, axis=0)).astype(bf16)
            summed = jnp.dot(mask, scaled, preferred_element_type=f32)
            total = total + jnp.concatenate(downs, axis=0) * summed
        inner[:, cols] = total
        return 0

    def entering_table(b, _):
        cols = pl.ds(pl.multiple_of(b * LANES, LANES), LANES)
        rate = rate_rows[pl.ds(b, 1), :]
        weight = weight_rows[pl.ds(b, 1), :]
        cross_table[:, cols] = jnp.where(linked, weight * jnp.exp(-rate * ahead), 0.0).astype(bf16)
        return 0

    half = wide_blocks // 2
    lax.fori_loop(0, half, conv, 0)

    width = chans // block
    slice_rate = chan_rate[:, pl.ds(pl.multiple_of(pos * width, width), width)]
    decay = jnp.exp(-slice_rate * float(tok))

    def keep_of(index):
        crossing = start_of(index * tok + tok - 1) < index * tok
        return jnp.where(crossing, 1.0, 0.0)[:, :1]

    for copy in first:
        copy.wait()
    carry = jnp.zeros(slice_rate.shape, f32)
    factor = jnp.ones(slice_rate.shape, f32)
    factors = []
    for e in range(block):
        prefix_buf[e] = carry
        factors.append(factor)
        step = keep_of(zone * block + e) * decay
        carry = step * carry + gather_buf[e].astype(f32)
        factor = step * factor
    exit_buf[...] = carry.astype(exit_buf.dtype)

    def onward(k):
        return pltpu.make_async_remote_copy(
            src_ref=exit_buf, dst_ref=far_buf.at[k - 1],
            send_sem=send2.at[k - 1], recv_sem=recv2.at[k - 1],
            device_id=where_is(me + k * block), device_id_type=MESH)

    for k in range(1, reach + 1):
        @pl.when(zone + k < block_count)
        def _(k=k):
            onward(k).start()

    lax.fori_loop(0, lane_blocks, entering_table, 0, unroll=4)

    for k in range(1, reach + 1):
        @pl.when(zone >= k)
        def _(k=k):
            onward(k).wait_recv()

        @pl.when(zone < k)
        def _(k=k):
            far_buf[k - 1] = jnp.zeros(far_buf.shape[1:], far_buf.dtype)

    last_start = start_of(jnp.maximum(zone * block * tok - 1, 0))
    far = jnp.zeros(slice_rate.shape, f32)
    for k in range(1, reach + 1):
        same = (last_start < (zone - k + 1) * block * tok)
        flag = jnp.where(same, 1.0, 0.0)[:, :1]
        scale = flag * jnp.exp(-slice_rate * float(tok * block * (k - 1)))
        far = far + scale * far_buf[k - 1].astype(f32)
    for e in range(block):
        reply_buf[e] = (prefix_buf[e] + factors[e] * far).astype(reply_buf.dtype)

    last = []
    for s, mate in enumerate(mates):
        last.append(pltpu.make_async_remote_copy(
            src_ref=reply_buf.at[(pos + s + 1) % block], dst_ref=enter_buf.at[pos],
            send_sem=send3.at[s], recv_sem=recv3.at[s],
            device_id=where_is(mate), device_id_type=MESH))
        last[-1].start()
    enter_buf[pos] = reply_buf[pos]

    lax.fori_loop(half, wide_blocks, conv, 0)
    loads[2].wait()
    for copy in last:
        copy.wait()

    def finish(b, _):
        cols = pl.ds(pl.multiple_of(b * LANES, LANES), LANES)
        state = enter_buf[b // per_slice, :, pl.ds(pl.multiple_of((b % per_slice) * LANES, LANES), LANES)].astype(f32)
        spread = jnp.where(diagonal, jnp.concatenate([state] * (LANES // modes), axis=0), 0.0).astype(bf16)
        cross = jnp.dot(cross_table[:, cols], spread, preferred_element_type=f32)
        smoothed = (inner[:, cols] + cross).astype(bf16)
        out_buf[:, cols] = q_buf[:, cols] * smoothed
        return 0

    lax.fori_loop(0, lane_blocks, finish, 0, unroll=4)
    store = pltpu.make_async_copy(out_buf, out_hbm, store_sem)
    store.start()
    for k in range(1, reach + 1):
        @pl.when(zone + k < block_count)
        def _(k=k):
            onward(k).wait_send()
    store.wait()


def shards(query_gate, key_gate, values, rate_mix, residue, skip_gain, doc_lengths):
    ctx_count = lax.axis_size("ctx")
    head_count = lax.axis_size("head")
    devices = ctx_count * head_count
    tok, chans = query_gate.shape
    groups, modes = rate_mix.shape
    group_width = chans // groups
    total_tokens = tok * devices
    longest = total_tokens // 4
    block = min(devices // 4, chans // (4 * LANES))
    reach = -(-longest // (tok * block))
    rate = jnp.exp(-math.log(30.0) - rate_mix * math.log(float(total_tokens)))
    weight = residue * jnp.sqrt(-jnp.expm1(-2.0 * rate))
    rate_rows = rate.reshape(-1, LANES)
    weight_rows = weight.reshape(-1, LANES)
    rate_chan = jnp.repeat(rate.T, group_width, axis=1)
    weight_chan = jnp.repeat(weight.T, group_width, axis=1)
    width = chans // block
    wire = bf16
    vmem = pl.BlockSpec(memory_space=pltpu.VMEM)
    anywhere = pl.BlockSpec(memory_space=pl.ANY)
    dma = pltpu.SemaphoreType.DMA
    return pl.pallas_call(
        functools.partial(kernel, (ctx_count, head_count, block, reach)),
        out_shape=jax.ShapeDtypeStruct((tok, chans), bf16),
        in_specs=[pl.BlockSpec(memory_space=pltpu.SMEM), anywhere, anywhere, anywhere] + [vmem] * 5,
        out_specs=anywhere,
        scratch_shapes=[
            pltpu.VMEM((tok, chans), bf16), pltpu.VMEM((tok, chans), bf16),
            pltpu.VMEM((tok, chans), bf16), pltpu.VMEM((tok, chans), bf16),
            pltpu.VMEM((tok, chans), bf16), pltpu.VMEM((tok, chans), f32),
            pltpu.VMEM((tok, chans), bf16),
            pltpu.VMEM((block, modes, width), wire),
            pltpu.VMEM((block, modes, width), wire),
            pltpu.VMEM((block, modes, width), f32),
            pltpu.VMEM((block, modes, width), wire),
            pltpu.VMEM((block, modes, width), wire),
            pltpu.VMEM((modes, width), wire),
            pltpu.VMEM((reach, modes, width), wire),
            dma((3,)), dma, dma((block - 1,)), dma((block - 1,)),
            dma((reach,)), dma((reach,)), dma((block - 1,)), dma((block - 1,)),
        ],
        compiler_params=pltpu.CompilerParams(collective_id=0, has_side_effects=True,
                                             vmem_limit_bytes=32 * 1024 * 1024),
    )(doc_lengths, query_gate, key_gate, values, rate_rows, weight_rows, rate_chan, weight_chan, skip_gain.reshape(1, -1))


def solution(mesh):
    spans = P(("ctx", "head"), None)
    return jax.shard_map(
        shards,
        mesh=mesh,
        in_specs=(spans, spans, spans, P(), P(), P(), P()),
        out_specs=spans,
        check_vma=False,
    )
```

```python
import functools
import math

import jax
import jax.numpy as jnp
from jax import lax
from jax.experimental import pallas as pl
from jax.experimental.pallas import tpu as pltpu
from jax.sharding import PartitionSpec as P

LANES = 128
MESH = pl.DeviceIdType.MESH
f32 = jnp.float32
bf16 = jnp.bfloat16


def doc_start(tokens, ends):
    start = jnp.zeros_like(tokens)
    for end in ends:
        start = jnp.maximum(start, jnp.where(tokens >= end, end, 0))
    return start


def split_three(x):
    high = x.astype(bf16)
    rest = x - high.astype(f32)
    middle = rest.astype(bf16)
    low = (rest - middle.astype(f32)).astype(bf16)
    return [high, middle, low]


def kernel(cfg, lengths, q_hbm, k_hbm, v_hbm, rate_mix, residue, skip,
           out_hbm, q_buf, k_buf, v_buf, out_buf, mixed, inner, cross_table,
           chan_rate, chan_weight, rate_row, weight_row,
           state_buf, gather_buf, prefix_buf, reply_buf, enter_buf, exit_buf, far_buf,
           load_sem, store_sem, send1, recv1, send2, recv2, send3, recv3):
    ctx_count, head_count, block, reach = cfg
    devices = ctx_count * head_count
    tok, chans = mixed.shape
    modes = chan_rate.shape[0]
    lane_blocks = chans // LANES
    per_slice = lane_blocks // block
    group_width = LANES * modes // LANES
    block_count = devices // block
    me = lax.axis_index("ctx") * head_count + lax.axis_index("head")
    zone, pos = me // block, me % block
    span = me * tok

    def where_is(index):
        return (index // head_count, index % head_count)

    loads = []
    for n, (src, dst) in enumerate(((k_hbm, k_buf), (v_hbm, v_buf), (q_hbm, q_buf))):
        loads.append(pltpu.make_async_copy(src, dst, load_sem.at[n]))
        loads[-1].start()

    barrier = pltpu.get_barrier_semaphore()
    mates = [zone * block + (pos + s) % block for s in range(1, block)]
    for mate in mates:
        pl.semaphore_signal(barrier, inc=1, device_id=where_is(mate), device_id_type=MESH)
    for k in range(1, reach + 1):
        @pl.when(zone + k < block_count)
        def _(k=k):
            pl.semaphore_signal(barrier, inc=1, device_id=where_is(me + k * block), device_id_type=MESH)

        @pl.when(zone >= k)
        def _(k=k):
            pl.semaphore_signal(barrier, inc=1, device_id=where_is(me - k * block), device_id_type=MESH)

    ends, total = [], jnp.int32(0)
    for n in range(lengths.shape[0]):
        total = total + lengths[n]
        ends.append(total)

    def start_of(token):
        return doc_start(jnp.full((1, LANES), token, jnp.int32), ends)

    rows = lax.broadcasted_iota(jnp.int32, (tok, LANES), 0)
    gr = lax.broadcasted_iota(jnp.int32, (LANES, LANES), 0) // modes
    gc = lax.broadcasted_iota(jnp.int32, (LANES, LANES), 1) // group_width
    diagonal = gr == gc

    rate = jnp.exp(-math.log(30.0) - rate_mix[...] * math.log(float(devices * tok)))
    double = 2.0 * rate
    one_minus = jnp.where(double < 1e-2,
                          double * (1.0 - double * (0.5 - double * (1.0 / 6.0 - double / 24.0))),
                          1.0 - jnp.exp(-double))
    weight = residue[...] * jnp.sqrt(one_minus)
    stacked = jnp.concatenate([p.astype(f32) for p in split_three(rate) + split_three(weight)], axis=0).astype(bf16)
    spread_to = LANES * group_width
    onto = jnp.where(lax.broadcasted_iota(jnp.int32, (LANES, spread_to), 0)
                     == lax.broadcasted_iota(jnp.int32, (LANES, spread_to), 1) // group_width, 1.0, 0.0).astype(bf16)
    own = (lax.broadcasted_iota(jnp.int32, (modes, spread_to), 0)
           == lax.broadcasted_iota(jnp.int32, (modes, spread_to), 1) % modes)
    for n in range(rate.shape[1] // LANES):
        wide_table = jnp.dot(stacked[:, n * LANES:(n + 1) * LANES], onto, preferred_element_type=f32)
        parts = [wide_table[m * modes:(m + 1) * modes] for m in range(6)]
        cols = slice(n * spread_to, (n + 1) * spread_to)
        for m, (table, row) in enumerate(((chan_rate, rate_row), (chan_weight, weight_row))):
            value = parts[3 * m] + (parts[3 * m + 1] + parts[3 * m + 2])
            table[:, cols] = value
            row[:, cols] = jnp.sum(jnp.where(own, value, 0.0), axis=0, keepdims=True)

    tail_start = start_of(span + tok - 1) - span
    tail = rows >= tail_start
    left = (tok - 1 - rows).astype(f32)

    loads[0].wait()
    loads[1].wait()

    def local(b, _):
        cols = pl.ds(pl.multiple_of(b * LANES, LANES), LANES)
        x = k_buf[:, cols] * v_buf[:, cols]
        mixed[:, cols] = x
        rate = rate_row[:, cols]
        table = jnp.where(tail, jnp.exp(-rate * left), 0.0).astype(bf16)
        full = lax.dot_general(table, x, (((0,), (0,)), ((), ())), preferred_element_type=f32)
        full = jnp.where(diagonal, full, 0.0)
        state = jnp.sum(full.reshape(LANES // modes, modes, LANES), axis=0)
        state_buf[b // per_slice, :, pl.ds(pl.multiple_of((b % per_slice) * LANES, LANES), LANES)] = state.astype(state_buf.dtype)
        return 0

    lax.fori_loop(0, lane_blocks, local, 0, unroll=4)

    expected = (block - 1)
    for k in range(1, reach + 1):
        expected = expected + jnp.where(zone + k < block_count, 1, 0) + jnp.where(zone >= k, 1, 0)
    pl.semaphore_wait(barrier, expected)

    first = []
    for s, mate in enumerate(mates):
        first.append(pltpu.make_async_remote_copy(
            src_ref=state_buf.at[(pos + s + 1) % block], dst_ref=gather_buf.at[pos],
            send_sem=send1.at[s], recv_sem=recv1.at[s],
            device_id=where_is(mate), device_id_type=MESH))
        first[-1].start()
    gather_buf[pos] = state_buf[pos]

    row_tok = span + rows
    row_start = doc_start(row_tok, ends) - span
    lane_iota = lax.broadcasted_iota(jnp.int32, (tok, tok), 1)
    row_iota = lax.broadcasted_iota(jnp.int32, (tok, tok), 0)
    mask = jnp.where((lane_iota >= row_start[:, :1]) & (lane_iota <= row_iota), 1.0, 0.0).astype(bf16)
    linked = row_start < 0
    ahead = (rows + 1).astype(f32)

    wide = 2 * LANES
    wide_blocks = chans // wide
    eights = lax.broadcasted_iota(jnp.int32, (8, wide), 0).astype(f32)

    def conv(b, _):
        cols = pl.ds(pl.multiple_of(b * wide, wide), wide)
        x = mixed[:, cols].astype(f32)
        total = skip[:, cols] * x
        for r in range(modes):
            rate = chan_rate[r:r + 1, cols]
            up = jnp.exp(rate * eights)
            down = chan_weight[r:r + 1, cols] * jnp.exp(-rate * eights)
            up_step = jnp.broadcast_to(jnp.exp(8.0 * rate), up.shape)
            down_step = jnp.broadcast_to(jnp.exp(-8.0 * rate), up.shape)
            ups, downs = [], []
            for _p in range(tok // 8):
                ups.append(up)
                downs.append(down)
                up, down = up * up_step, down * down_step
            scaled = (x * jnp.concatenate(ups, axis=0)).astype(bf16)
            summed = jnp.dot(mask, scaled, preferred_element_type=f32)
            total = total + jnp.concatenate(downs, axis=0) * summed
        inner[:, cols] = total
        return 0

    def entering_table(b, _):
        cols = pl.ds(pl.multiple_of(b * LANES, LANES), LANES)
        rate = rate_row[:, cols]
        weight = weight_row[:, cols]
        cross_table[:, cols] = jnp.where(linked, weight * jnp.exp(-rate * ahead), 0.0).astype(bf16)
        return 0

    half = wide_blocks // 2
    lax.fori_loop(0, half, conv, 0)

    width = chans // block
    slice_rate = chan_rate[:, pl.ds(pl.multiple_of(pos * width, width), width)]
    decay = jnp.exp(-slice_rate * float(tok))

    def keep_of(index):
        crossing = start_of(index * tok + tok - 1) < index * tok
        return jnp.where(crossing, 1.0, 0.0)[:, :1]

    for copy in first:
        copy.wait()
    carry = jnp.zeros(slice_rate.shape, f32)
    factor = jnp.ones(slice_rate.shape, f32)
    factors = []
    for e in range(block):
        prefix_buf[e] = carry
        factors.append(factor)
        step = keep_of(zone * block + e) * decay
        carry = step * carry + gather_buf[e].astype(f32)
        factor = step * factor
    exit_buf[...] = carry.astype(exit_buf.dtype)

    def onward(k):
        return pltpu.make_async_remote_copy(
            src_ref=exit_buf, dst_ref=far_buf.at[k - 1],
            send_sem=send2.at[k - 1], recv_sem=recv2.at[k - 1],
            device_id=where_is(me + k * block), device_id_type=MESH)

    for k in range(1, reach + 1):
        @pl.when(zone + k < block_count)
        def _(k=k):
            onward(k).start()

    lax.fori_loop(0, lane_blocks, entering_table, 0, unroll=4)

    for k in range(1, reach + 1):
        @pl.when(zone >= k)
        def _(k=k):
            onward(k).wait_recv()

        @pl.when(zone < k)
        def _(k=k):
            far_buf[k - 1] = jnp.zeros(far_buf.shape[1:], far_buf.dtype)

    last_start = start_of(jnp.maximum(zone * block * tok - 1, 0))
    far = jnp.zeros(slice_rate.shape, f32)
    for k in range(1, reach + 1):
        same = (last_start < (zone - k + 1) * block * tok)
        flag = jnp.where(same, 1.0, 0.0)[:, :1]
        scale = flag * jnp.exp(-slice_rate * float(tok * block * (k - 1)))
        far = far + scale * far_buf[k - 1].astype(f32)
    for e in range(block):
        reply_buf[e] = (prefix_buf[e] + factors[e] * far).astype(reply_buf.dtype)

    last = []
    for s, mate in enumerate(mates):
        last.append(pltpu.make_async_remote_copy(
            src_ref=reply_buf.at[(pos + s + 1) % block], dst_ref=enter_buf.at[pos],
            send_sem=send3.at[s], recv_sem=recv3.at[s],
            device_id=where_is(mate), device_id_type=MESH))
        last[-1].start()
    enter_buf[pos] = reply_buf[pos]

    lax.fori_loop(half, wide_blocks, conv, 0)
    loads[2].wait()
    for copy in last:
        copy.wait()

    def finish(b, _):
        cols = pl.ds(pl.multiple_of(b * LANES, LANES), LANES)
        state = enter_buf[b // per_slice, :, pl.ds(pl.multiple_of((b % per_slice) * LANES, LANES), LANES)].astype(f32)
        spread = jnp.where(diagonal, jnp.concatenate([state] * (LANES // modes), axis=0), 0.0).astype(bf16)
        cross = jnp.dot(cross_table[:, cols], spread, preferred_element_type=f32)
        smoothed = (inner[:, cols] + cross).astype(bf16)
        out_buf[:, cols] = q_buf[:, cols] * smoothed
        return 0

    lax.fori_loop(0, lane_blocks, finish, 0, unroll=4)
    store = pltpu.make_async_copy(out_buf, out_hbm, store_sem)
    store.start()
    for k in range(1, reach + 1):
        @pl.when(zone + k < block_count)
        def _(k=k):
            onward(k).wait_send()
    store.wait()


def shards(query_gate, key_gate, values, rate_mix, residue, skip_gain, doc_lengths):
    ctx_count = lax.axis_size("ctx")
    head_count = lax.axis_size("head")
    devices = ctx_count * head_count
    tok, chans = query_gate.shape
    groups, modes = rate_mix.shape
    group_width = chans // groups
    total_tokens = tok * devices
    longest = total_tokens // 4
    block = min(devices // 4, chans // (4 * LANES))
    reach = -(-longest // (tok * block))
    width = chans // block
    wire = bf16
    vmem = pl.BlockSpec(memory_space=pltpu.VMEM)
    hbm = pl.BlockSpec(memory_space=pltpu.HBM)
    dma = pltpu.SemaphoreType.DMA
    return pl.pallas_call(
        functools.partial(kernel, (ctx_count, head_count, block, reach)),
        out_shape=jax.ShapeDtypeStruct((tok, chans), bf16),
        in_specs=[pl.BlockSpec(memory_space=pltpu.SMEM), hbm, hbm, hbm, vmem, vmem, vmem],
        out_specs=hbm,
        scratch_shapes=[
            pltpu.VMEM((tok, chans), bf16), pltpu.VMEM((tok, chans), bf16),
            pltpu.VMEM((tok, chans), bf16), pltpu.VMEM((tok, chans), bf16),
            pltpu.VMEM((tok, chans), bf16), pltpu.VMEM((tok, chans), f32),
            pltpu.VMEM((tok, chans), bf16),
            pltpu.VMEM((modes, chans), f32), pltpu.VMEM((modes, chans), f32),
            pltpu.VMEM((1, chans), f32), pltpu.VMEM((1, chans), f32),
            pltpu.VMEM((block, modes, width), wire),
            pltpu.VMEM((block, modes, width), wire),
            pltpu.VMEM((block, modes, width), f32),
            pltpu.VMEM((block, modes, width), wire),
            pltpu.VMEM((block, modes, width), wire),
            pltpu.VMEM((modes, width), wire),
            pltpu.VMEM((reach, modes, width), wire),
            dma((3,)), dma, dma((block - 1,)), dma((block - 1,)),
            dma((reach,)), dma((reach,)), dma((block - 1,)), dma((block - 1,)),
        ],
        compiler_params=pltpu.CompilerParams(collective_id=0, has_side_effects=True),
    )(doc_lengths, query_gate, key_gate, values, rate_mix.T, residue.T, skip_gain.reshape(1, -1))


def solution(mesh):
    spans = P(("ctx", "head"), None)
    return jax.shard_map(
        shards,
        mesh=mesh,
        in_specs=(spans, spans, spans, P(), P(), P(), P()),
        out_specs=spans,
        check_vma=False,
    )
```

```python
import functools
import math

import jax
import jax.numpy as jnp
from jax import lax
from jax.experimental import pallas as pl
from jax.experimental.pallas import tpu as pltpu
from jax.sharding import PartitionSpec as P

LANES = 128
EARLY = 3
CUTS = (7, 10)
MESH = pl.DeviceIdType.MESH
f32 = jnp.float32
bf16 = jnp.bfloat16


def doc_start(tokens, ends):
    start = jnp.zeros_like(tokens)
    for end in ends:
        start = jnp.maximum(start, jnp.where(tokens >= end, end, 0))
    return start


def split_three(x):
    high = x.astype(bf16)
    rest = x - high.astype(f32)
    middle = rest.astype(bf16)
    low = (rest - middle.astype(f32)).astype(bf16)
    return [high, middle, low]


def kernel(cfg, lengths, k_hbm, v_hbm, rate_mix, residue, skip,
           inner_hbm, table_hbm, enter_hbm, k_buf, v_buf, mixed, inner, cross_table,
           chan_rate, chan_weight, rate_row, weight_row,
           state_buf, gather_buf, prefix_buf, factor_buf, reply_buf, exit_buf, far_buf,
           load_sem, inner_sem, table_sem, own_sem, send1, recv1, send2, recv2, send3, recv3):
    ctx_count, head_count, block, reach = cfg
    devices = ctx_count * head_count
    tok, chans = mixed.shape
    modes = chan_rate.shape[0]
    lane_blocks = chans // LANES
    per_slice = lane_blocks // block
    group_width = LANES * modes // LANES
    block_count = devices // block
    me = lax.axis_index("ctx") * head_count + lax.axis_index("head")
    zone, pos = me // block, me % block
    span = me * tok

    def where_is(index):
        return (index // head_count, index % head_count)

    width = chans // block

    def mate_of(s):
        mate, bit = 0, 1
        while bit < block:
            mine = (pos // bit) % 2
            mate = mate + (1 - mine if s & bit else mine) * bit
            bit *= 2
        return mate

    order = sorted(range(block), key=lambda s: (-(s & ~head_count).bit_count(), s == 0))
    mates = {s: mate_of(s) for s in order}
    loads = {}
    for s in order:
        cols = pl.ds(pl.multiple_of(mates[s] * width, width), width)
        loads[s] = [pltpu.make_async_copy(src.at[:, cols], dst.at[:, cols], load_sem.at[n, s])
                    for n, (src, dst) in enumerate(((k_hbm, k_buf), (v_hbm, v_buf)))]
        for load in loads[s]:
            load.start()

    barrier = pltpu.get_barrier_semaphore()
    for s in order:
        if s:
            pl.semaphore_signal(barrier, inc=1, device_id=where_is(zone * block + mates[s]), device_id_type=MESH)
    for k in range(1, reach + 1):
        @pl.when(zone + k < block_count)
        def _(k=k):
            pl.semaphore_signal(barrier, inc=1, device_id=where_is(me + k * block), device_id_type=MESH)

        @pl.when(zone >= k)
        def _(k=k):
            pl.semaphore_signal(barrier, inc=1, device_id=where_is(me - k * block), device_id_type=MESH)

    ends, total = [], jnp.int32(0)
    for n in range(lengths.shape[0]):
        total = total + lengths[n]
        ends.append(total)

    def start_of(token):
        return doc_start(jnp.full((modes, LANES), token, jnp.int32), ends)

    rows = lax.broadcasted_iota(jnp.int32, (tok, LANES), 0)
    gr = lax.broadcasted_iota(jnp.int32, (LANES, LANES), 0) // modes
    gc = lax.broadcasted_iota(jnp.int32, (LANES, LANES), 1) // group_width
    diagonal = gr == gc

    rate = jnp.exp(-math.log(30.0) - rate_mix[...] * math.log(float(devices * tok)))
    double = 2.0 * rate
    one_minus = jnp.where(double < 1e-2,
                          double * (1.0 - double * (0.5 - double * (1.0 / 6.0 - double / 24.0))),
                          1.0 - jnp.exp(-double))
    weight = residue[...] * jnp.sqrt(one_minus)
    stacked = jnp.concatenate([p.astype(f32) for p in split_three(rate) + split_three(weight)], axis=0).astype(bf16)
    spread_to = LANES * group_width
    onto = jnp.where(lax.broadcasted_iota(jnp.int32, (LANES, spread_to), 0)
                     == lax.broadcasted_iota(jnp.int32, (LANES, spread_to), 1) // group_width, 1.0, 0.0).astype(bf16)
    own = (lax.broadcasted_iota(jnp.int32, (modes, spread_to), 0)
           == lax.broadcasted_iota(jnp.int32, (modes, spread_to), 1) % modes)
    for n in range(rate.shape[1] // LANES):
        wide_table = jnp.dot(stacked[:, n * LANES:(n + 1) * LANES], onto, preferred_element_type=f32)
        parts = [wide_table[m * modes:(m + 1) * modes] for m in range(6)]
        cols = slice(n * spread_to, (n + 1) * spread_to)
        for m, (table, row) in enumerate(((chan_rate, rate_row), (chan_weight, weight_row))):
            value = parts[3 * m] + (parts[3 * m + 1] + parts[3 * m + 2])
            table[:, cols] = value
            row[:, cols] = jnp.sum(jnp.where(own, value, 0.0), axis=0, keepdims=True)

    tail_start = start_of(span + tok - 1)[:1] - span
    tail = rows >= tail_start
    left = (tok - 1 - rows).astype(f32)

    expected = block - 1
    for k in range(1, reach + 1):
        expected = expected + jnp.where(zone + k < block_count, 1, 0) + jnp.where(zone >= k, 1, 0)

    def local(s):
        for load in loads[s]:
            load.wait()
        for i in range(per_slice):
            cols = pl.ds(pl.multiple_of(mates[s] * width + i * LANES, LANES), LANES)
            x = k_buf[:, cols] * v_buf[:, cols]
            mixed[:, cols] = x
            rate = rate_row[:, cols]
            table = jnp.where(tail, jnp.exp(-rate * left), 0.0).astype(bf16)
            full = lax.dot_general(table, x, (((0,), (0,)), ((), ())), preferred_element_type=f32)
            full = jnp.where(diagonal, full, 0.0)
            state = jnp.sum(full.reshape(LANES // modes, modes, LANES), axis=0)
            state_buf[mates[s], :, i * LANES:(i + 1) * LANES] = state.astype(state_buf.dtype)

    first = {s: pltpu.make_async_remote_copy(
        src_ref=state_buf.at[mates[s]], dst_ref=gather_buf.at[pos],
        send_sem=send1.at[s - 1], recv_sem=recv1.at[s - 1],
        device_id=where_is(zone * block + mates[s]), device_id_type=MESH) for s in order if s}

    early = order[:EARLY]
    for s in early:
        local(s)
    pl.semaphore_wait(barrier, expected)
    for s in early:
        first[s].start()
    for s in order[EARLY:]:
        local(s)
        if s:
            first[s].start()
    gather_buf[pos] = state_buf[pos]

    row_tok = span + rows
    row_start = doc_start(row_tok, ends) - span
    lane_iota = lax.broadcasted_iota(jnp.int32, (tok, tok), 1)
    row_iota = lax.broadcasted_iota(jnp.int32, (tok, tok), 0)
    mask = jnp.where((lane_iota >= row_start[:, :1]) & (lane_iota <= row_iota), 1.0, 0.0).astype(bf16)
    linked = row_start < 0
    ahead = (rows + 1).astype(f32)

    wide = 2 * LANES
    wide_blocks = chans // wide
    eights = lax.broadcasted_iota(jnp.int32, (8, wide), 0).astype(f32)

    def conv(b, _):
        cols = pl.ds(pl.multiple_of(b * wide, wide), wide)
        x = mixed[:, cols].astype(f32)
        total = skip[:, cols] * x
        for r in range(modes):
            rate = chan_rate[r:r + 1, cols]
            up = jnp.exp(rate * eights)
            down = chan_weight[r:r + 1, cols] * jnp.exp(-rate * eights)
            up_step = jnp.broadcast_to(jnp.exp(8.0 * rate), up.shape)
            down_step = jnp.broadcast_to(jnp.exp(-8.0 * rate), up.shape)
            ups, downs = [], []
            for _p in range(tok // 8):
                ups.append(up)
                downs.append(down)
                up, down = up * up_step, down * down_step
            scaled = (x * jnp.concatenate(ups, axis=0)).astype(bf16)
            summed = jnp.dot(mask, scaled, preferred_element_type=f32)
            total = total + jnp.concatenate(downs, axis=0) * summed
        inner[:, cols] = total.astype(inner.dtype)
        pltpu.make_async_copy(inner.at[:, cols], inner_hbm.at[:, cols], inner_sem.at[b]).start()
        return 0

    def entering_table(b, _):
        cols = pl.ds(pl.multiple_of(b * LANES, LANES), LANES)
        rate = rate_row[:, cols]
        weight = weight_row[:, cols]
        cross_table[:, cols] = jnp.where(linked, weight * jnp.exp(-rate * ahead), 0.0).astype(bf16)
        return 0

    cut1, cut2 = wide_blocks * CUTS[0] // 16, wide_blocks * CUTS[1] // 16
    lax.fori_loop(0, cut1, conv, 0)
    lax.fori_loop(0, lane_blocks, entering_table, 0, unroll=4)
    table_store = pltpu.make_async_copy(cross_table, table_hbm, table_sem)
    table_store.start()

    slice_rate = chan_rate[:, pl.ds(pl.multiple_of(pos * width, width), width)]
    decay = jnp.exp(-slice_rate * float(tok))

    def repeat_lanes(row):
        return jnp.concatenate([row] * (width // LANES), axis=1)

    def keep_of(index):
        crossing = start_of(index * tok + tok - 1) < index * tok
        return repeat_lanes(jnp.where(crossing, 1.0, 0.0))

    keeps = [keep_of(zone * block + e) * decay for e in range(block)]
    last_start = start_of(jnp.maximum(zone * block * tok - 1, 0))

    for copy in first.values():
        copy.wait()
    carry = jnp.zeros(slice_rate.shape, f32)
    factor = jnp.ones(slice_rate.shape, f32)
    for e in range(block):
        prefix_buf[e] = carry
        factor_buf[e] = factor
        step = keeps[e]
        carry = step * carry + gather_buf[e].astype(f32)
        factor = step * factor
    exit_buf[...] = carry.astype(exit_buf.dtype)

    def onward(k):
        return pltpu.make_async_remote_copy(
            src_ref=exit_buf, dst_ref=far_buf.at[k - 1],
            send_sem=send2.at[k - 1], recv_sem=recv2.at[k - 1],
            device_id=where_is(me + k * block), device_id_type=MESH)

    for k in range(1, reach + 1):
        @pl.when(zone + k < block_count)
        def _(k=k):
            onward(k).start()

    lax.fori_loop(cut1, cut2, conv, 0)

    for k in range(1, reach + 1):
        @pl.when(zone >= k)
        def _(k=k):
            onward(k).wait_recv()

        @pl.when(zone < k)
        def _(k=k):
            far_buf[k - 1] = jnp.zeros(far_buf.shape[1:], far_buf.dtype)

    far = jnp.zeros(slice_rate.shape, f32)
    for k in range(1, reach + 1):
        same = (last_start < (zone - k + 1) * block * tok)
        flag = repeat_lanes(jnp.where(same, 1.0, 0.0))
        scale = flag * jnp.exp(-slice_rate * float(tok * block * (k - 1)))
        far = far + scale * far_buf[k - 1].astype(f32)
    last = {s: pltpu.make_async_remote_copy(
        src_ref=reply_buf.at[mates[s]], dst_ref=enter_hbm.at[pos],
        send_sem=send3.at[s - 1], recv_sem=recv3.at[s - 1],
        device_id=where_is(zone * block + mates[s]), device_id_type=MESH) for s in order if s}
    for s in order:
        reply_buf[mates[s]] = (prefix_buf[mates[s]] + factor_buf[mates[s]] * far).astype(reply_buf.dtype)
        if s:
            last[s].start()
    own_copy = pltpu.make_async_copy(reply_buf.at[pos], enter_hbm.at[pos], own_sem)
    own_copy.start()

    lax.fori_loop(cut2, wide_blocks, conv, 0)

    for k in range(1, reach + 1):
        @pl.when(zone + k < block_count)
        def _(k=k):
            onward(k).wait_send()
    table_store.wait()

    def stored(b, _):
        cols = pl.ds(pl.multiple_of(b * wide, wide), wide)
        pltpu.make_async_copy(inner.at[:, cols], inner_hbm.at[:, cols], inner_sem.at[b]).wait()
        return 0

    lax.fori_loop(0, wide_blocks, stored, 0)
    own_copy.wait()
    for copy in last.values():
        copy.wait()


def finish_kernel(q_hbm, inner_hbm, table_hbm, enter_hbm, out_hbm,
                  q_buf, inner, table, enter, out_buf, enter_sem, load_sem, store_sem):
    tok, chans = q_buf.shape
    block, modes, width = enter.shape
    group_width = modes
    entering = pltpu.make_async_copy(enter_hbm, enter, enter_sem)
    entering.start()
    loads = []
    for e in range(block):
        cols = slice(e * width, (e + 1) * width)
        loads.append([pltpu.make_async_copy(src.at[:, cols], dst.at[:, cols], load_sem.at[n, e])
                      for n, (src, dst) in enumerate(((q_hbm, q_buf), (inner_hbm, inner), (table_hbm, table)))])
        for load in loads[e]:
            load.start()
    diagonal = (lax.broadcasted_iota(jnp.int32, (LANES, LANES), 0) // modes
                == lax.broadcasted_iota(jnp.int32, (LANES, LANES), 1) // group_width)
    entering.wait()
    stores = []
    for e in range(block):
        for load in loads[e]:
            load.wait()
        for i in range(width // LANES):
            cols = slice(e * width + i * LANES, e * width + (i + 1) * LANES)
            state = enter[e, :, i * LANES:(i + 1) * LANES].astype(f32)
            spread = jnp.where(diagonal, jnp.concatenate([state] * (LANES // modes), axis=0), 0.0).astype(bf16)
            cross = jnp.dot(table[:, cols], spread, preferred_element_type=f32)
            smoothed = (inner[:, cols].astype(f32) + cross).astype(bf16)
            out_buf[:, cols] = q_buf[:, cols] * smoothed
        cols = slice(e * width, (e + 1) * width)
        stores.append(pltpu.make_async_copy(out_buf.at[:, cols], out_hbm.at[:, cols], store_sem.at[e]))
        stores[e].start()
    for store in stores:
        store.wait()


def shards(query_gate, key_gate, values, rate_mix, residue, skip_gain, doc_lengths):
    ctx_count = lax.axis_size("ctx")
    head_count = lax.axis_size("head")
    devices = ctx_count * head_count
    tok, chans = query_gate.shape
    groups, modes = rate_mix.shape
    group_width = chans // groups
    total_tokens = tok * devices
    longest = total_tokens // 4
    block = min(devices // 4, chans // (4 * LANES))
    reach = -(-longest // (tok * block))
    width = chans // block
    wire = bf16
    vmem = pl.BlockSpec(memory_space=pltpu.VMEM)
    hbm = pl.BlockSpec(memory_space=pltpu.HBM)
    dma = pltpu.SemaphoreType.DMA
    whole = pltpu.VMEM((tok, chans), bf16)
    slices = pltpu.VMEM((block, modes, width), wire)
    inner, table, enter = pl.pallas_call(
        functools.partial(kernel, (ctx_count, head_count, block, reach)),
        out_shape=(jax.ShapeDtypeStruct((tok, chans), bf16), jax.ShapeDtypeStruct((tok, chans), bf16),
                   jax.ShapeDtypeStruct((block, modes, width), wire)),
        in_specs=[pl.BlockSpec(memory_space=pltpu.SMEM), hbm, hbm, vmem, vmem, vmem],
        out_specs=(hbm, hbm, hbm),
        scratch_shapes=[
            whole, whole, whole, whole, whole,
            pltpu.VMEM((modes, chans), f32), pltpu.VMEM((modes, chans), f32),
            pltpu.VMEM((1, chans), f32), pltpu.VMEM((1, chans), f32),
            slices, slices,
            pltpu.VMEM((block, modes, width), f32), pltpu.VMEM((block, modes, width), f32),
            slices,
            pltpu.VMEM((modes, width), wire),
            pltpu.VMEM((reach, modes, width), wire),
            dma((2, block)), dma((chans // (2 * LANES),)), dma, dma,
            dma((block - 1,)), dma((block - 1,)),
            dma((reach,)), dma((reach,)), dma((block - 1,)), dma((block - 1,)),
        ],
        compiler_params=pltpu.CompilerParams(collective_id=0, has_side_effects=True),
    )(doc_lengths, key_gate, values, rate_mix.T, residue.T, skip_gain.reshape(1, -1))
    return pl.pallas_call(
        finish_kernel,
        out_shape=jax.ShapeDtypeStruct((tok, chans), bf16),
        in_specs=[hbm] * 4,
        out_specs=hbm,
        scratch_shapes=[whole, whole, whole, slices, whole, dma, dma((3, block)), dma((block,))],
    )(query_gate, inner, table, enter)


def solution(mesh):
    spans = P(("ctx", "head"), None)
    return jax.shard_map(
        shards,
        mesh=mesh,
        in_specs=(spans, spans, spans, P(), P(), P(), P()),
        out_specs=spans,
        check_vma=False,
    )
```

```python
import functools
import math

import jax
import jax.numpy as jnp
from jax import lax
from jax.experimental import pallas as pl
from jax.experimental.pallas import tpu as pltpu
from jax.sharding import PartitionSpec as P

LANES = 128
EARLY = 3
CUTS = (7, 10)
MESH = pl.DeviceIdType.MESH
f32 = jnp.float32
bf16 = jnp.bfloat16


def doc_start(tokens, ends):
    start = jnp.zeros_like(tokens)
    for end in ends:
        start = jnp.maximum(start, jnp.where(tokens >= end, end, 0))
    return start


def split_three(x):
    high = x.astype(bf16)
    rest = x - high.astype(f32)
    middle = rest.astype(bf16)
    low = (rest - middle.astype(f32)).astype(bf16)
    return [high, middle, low]


def kernel(cfg, lengths, q_hbm, k_hbm, v_hbm, rate_mix, residue, skip,
           out_buf, q_buf, k_buf, v_buf, mixed, inner, cross_table,
           chan_rate, chan_weight, rate_row, weight_row,
           state_buf, gather_buf, prefix_buf, factor_buf, reply_buf, enter_buf, exit_buf, far_buf,
           load_sem, q_sem, send1, recv1, send2, recv2, send3, recv3):
    ctx_count, head_count, block, reach = cfg
    devices = ctx_count * head_count
    tok, chans = mixed.shape
    modes = chan_rate.shape[0]
    lane_blocks = chans // LANES
    per_slice = lane_blocks // block
    group_width = LANES * modes // LANES
    block_count = devices // block
    me = lax.axis_index("ctx") * head_count + lax.axis_index("head")
    zone, pos = me // block, me % block
    span = me * tok

    def where_is(index):
        return (index // head_count, index % head_count)

    width = chans // block

    def mate_of(s):
        mate, bit = 0, 1
        while bit < block:
            mine = (pos // bit) % 2
            mate = mate + (1 - mine if s & bit else mine) * bit
            bit *= 2
        return mate

    order = sorted(range(block), key=lambda s: (-(s & ~head_count).bit_count(), s == 0))
    mates = {s: mate_of(s) for s in order}
    loads = {}
    for s in order:
        cols = pl.ds(pl.multiple_of(mates[s] * width, width), width)
        loads[s] = [pltpu.make_async_copy(src.at[:, cols], dst.at[:, cols], load_sem.at[n, s])
                    for n, (src, dst) in enumerate(((k_hbm, k_buf), (v_hbm, v_buf)))]
        for load in loads[s]:
            load.start()
    q_load = pltpu.make_async_copy(q_hbm, q_buf, q_sem)
    q_load.start()

    barrier = pltpu.get_barrier_semaphore()
    for s in order:
        if s:
            pl.semaphore_signal(barrier, inc=1, device_id=where_is(zone * block + mates[s]), device_id_type=MESH)
    for k in range(1, reach + 1):
        @pl.when(zone + k < block_count)
        def _(k=k):
            pl.semaphore_signal(barrier, inc=1, device_id=where_is(me + k * block), device_id_type=MESH)

        @pl.when(zone >= k)
        def _(k=k):
            pl.semaphore_signal(barrier, inc=1, device_id=where_is(me - k * block), device_id_type=MESH)

    ends, total = [], jnp.int32(0)
    for n in range(lengths.shape[0]):
        total = total + lengths[n]
        ends.append(total)

    def start_of(token):
        return doc_start(jnp.full((modes, LANES), token, jnp.int32), ends)

    rows = lax.broadcasted_iota(jnp.int32, (tok, LANES), 0)
    gr = lax.broadcasted_iota(jnp.int32, (LANES, LANES), 0) // modes
    gc = lax.broadcasted_iota(jnp.int32, (LANES, LANES), 1) // group_width
    diagonal = gr == gc

    rate = jnp.exp(-math.log(30.0) - rate_mix[...] * math.log(float(devices * tok)))
    double = 2.0 * rate
    one_minus = jnp.where(double < 1e-2,
                          double * (1.0 - double * (0.5 - double * (1.0 / 6.0 - double / 24.0))),
                          1.0 - jnp.exp(-double))
    weight = residue[...] * jnp.sqrt(one_minus)
    stacked = jnp.concatenate([p.astype(f32) for p in split_three(rate) + split_three(weight)], axis=0).astype(bf16)
    spread_to = LANES * group_width
    onto = jnp.where(lax.broadcasted_iota(jnp.int32, (LANES, spread_to), 0)
                     == lax.broadcasted_iota(jnp.int32, (LANES, spread_to), 1) // group_width, 1.0, 0.0).astype(bf16)
    own = (lax.broadcasted_iota(jnp.int32, (modes, spread_to), 0)
           == lax.broadcasted_iota(jnp.int32, (modes, spread_to), 1) % modes)
    for n in range(rate.shape[1] // LANES):
        wide_table = jnp.dot(stacked[:, n * LANES:(n + 1) * LANES], onto, preferred_element_type=f32)
        parts = [wide_table[m * modes:(m + 1) * modes] for m in range(6)]
        cols = slice(n * spread_to, (n + 1) * spread_to)
        for m, (table, row) in enumerate(((chan_rate, rate_row), (chan_weight, weight_row))):
            value = parts[3 * m] + (parts[3 * m + 1] + parts[3 * m + 2])
            table[:, cols] = value
            row[:, cols] = jnp.sum(jnp.where(own, value, 0.0), axis=0, keepdims=True)

    tail_start = start_of(span + tok - 1)[:1] - span
    tail = rows >= tail_start
    left = (tok - 1 - rows).astype(f32)

    expected = block - 1
    for k in range(1, reach + 1):
        expected = expected + jnp.where(zone + k < block_count, 1, 0) + jnp.where(zone >= k, 1, 0)

    def local(s):
        for load in loads[s]:
            load.wait()
        for i in range(per_slice):
            cols = pl.ds(pl.multiple_of(mates[s] * width + i * LANES, LANES), LANES)
            x = k_buf[:, cols] * v_buf[:, cols]
            mixed[:, cols] = x
            rate = rate_row[:, cols]
            table = jnp.where(tail, jnp.exp(-rate * left), 0.0).astype(bf16)
            full = lax.dot_general(table, x, (((0,), (0,)), ((), ())), preferred_element_type=f32)
            full = jnp.where(diagonal, full, 0.0)
            state = jnp.sum(full.reshape(LANES // modes, modes, LANES), axis=0)
            state_buf[mates[s], :, i * LANES:(i + 1) * LANES] = state.astype(state_buf.dtype)

    first = {s: pltpu.make_async_remote_copy(
        src_ref=state_buf.at[mates[s]], dst_ref=gather_buf.at[pos],
        send_sem=send1.at[s - 1], recv_sem=recv1.at[s - 1],
        device_id=where_is(zone * block + mates[s]), device_id_type=MESH) for s in order if s}

    early = order[:EARLY]
    for s in early:
        local(s)
    pl.semaphore_wait(barrier, expected)
    for s in early:
        first[s].start()
    for s in order[EARLY:]:
        local(s)
        if s:
            first[s].start()
    gather_buf[pos] = state_buf[pos]

    row_tok = span + rows
    row_start = doc_start(row_tok, ends) - span
    lane_iota = lax.broadcasted_iota(jnp.int32, (tok, tok), 1)
    row_iota = lax.broadcasted_iota(jnp.int32, (tok, tok), 0)
    mask = jnp.where((lane_iota >= row_start[:, :1]) & (lane_iota <= row_iota), 1.0, 0.0).astype(bf16)
    linked = row_start < 0
    ahead = (rows + 1).astype(f32)

    wide = 2 * LANES
    wide_blocks = chans // wide
    eights = lax.broadcasted_iota(jnp.int32, (8, wide), 0).astype(f32)

    def conv(b, _):
        cols = pl.ds(pl.multiple_of(b * wide, wide), wide)
        x = mixed[:, cols].astype(f32)
        total = skip[:, cols] * x
        for r in range(modes):
            rate = chan_rate[r:r + 1, cols]
            up = jnp.exp(rate * eights)
            down = chan_weight[r:r + 1, cols] * jnp.exp(-rate * eights)
            up_step = jnp.broadcast_to(jnp.exp(8.0 * rate), up.shape)
            down_step = jnp.broadcast_to(jnp.exp(-8.0 * rate), up.shape)
            ups, downs = [], []
            for _p in range(tok // 8):
                ups.append(up)
                downs.append(down)
                up, down = up * up_step, down * down_step
            scaled = (x * jnp.concatenate(ups, axis=0)).astype(bf16)
            summed = jnp.dot(mask, scaled, preferred_element_type=f32)
            total = total + jnp.concatenate(downs, axis=0) * summed
        inner[:, cols] = total
        return 0

    def entering_table(b, _):
        cols = pl.ds(pl.multiple_of(b * LANES, LANES), LANES)
        rate = rate_row[:, cols]
        weight = weight_row[:, cols]
        cross_table[:, cols] = jnp.where(linked, weight * jnp.exp(-rate * ahead), 0.0).astype(bf16)
        return 0

    cut1, cut2 = wide_blocks * CUTS[0] // 16, wide_blocks * CUTS[1] // 16
    lax.fori_loop(0, cut1, conv, 0)
    lax.fori_loop(0, lane_blocks, entering_table, 0, unroll=4)

    slice_rate = chan_rate[:, pl.ds(pl.multiple_of(pos * width, width), width)]
    decay = jnp.exp(-slice_rate * float(tok))

    def repeat_lanes(row):
        return jnp.concatenate([row] * (width // LANES), axis=1)

    def keep_of(index):
        crossing = start_of(index * tok + tok - 1) < index * tok
        return repeat_lanes(jnp.where(crossing, 1.0, 0.0))

    keeps = [keep_of(zone * block + e) * decay for e in range(block)]
    last_start = start_of(jnp.maximum(zone * block * tok - 1, 0))

    for copy in first.values():
        copy.wait()
    carry = jnp.zeros(slice_rate.shape, f32)
    factor = jnp.ones(slice_rate.shape, f32)
    for e in range(block):
        prefix_buf[e] = carry
        factor_buf[e] = factor
        step = keeps[e]
        carry = step * carry + gather_buf[e].astype(f32)
        factor = step * factor
    exit_buf[...] = carry.astype(exit_buf.dtype)

    def onward(k):
        return pltpu.make_async_remote_copy(
            src_ref=exit_buf, dst_ref=far_buf.at[k - 1],
            send_sem=send2.at[k - 1], recv_sem=recv2.at[k - 1],
            device_id=where_is(me + k * block), device_id_type=MESH)

    for k in range(1, reach + 1):
        @pl.when(zone + k < block_count)
        def _(k=k):
            onward(k).start()

    lax.fori_loop(cut1, cut2, conv, 0)

    for k in range(1, reach + 1):
        @pl.when(zone >= k)
        def _(k=k):
            onward(k).wait_recv()

        @pl.when(zone < k)
        def _(k=k):
            far_buf[k - 1] = jnp.zeros(far_buf.shape[1:], far_buf.dtype)

    far = jnp.zeros(slice_rate.shape, f32)
    for k in range(1, reach + 1):
        same = (last_start < (zone - k + 1) * block * tok)
        flag = repeat_lanes(jnp.where(same, 1.0, 0.0))
        scale = flag * jnp.exp(-slice_rate * float(tok * block * (k - 1)))
        far = far + scale * far_buf[k - 1].astype(f32)
    last = {s: pltpu.make_async_remote_copy(
        src_ref=reply_buf.at[mates[s]], dst_ref=enter_buf.at[pos],
        send_sem=send3.at[s - 1], recv_sem=recv3.at[s - 1],
        device_id=where_is(zone * block + mates[s]), device_id_type=MESH) for s in order if s}
    for s in order:
        reply_buf[mates[s]] = (prefix_buf[mates[s]] + factor_buf[mates[s]] * far).astype(reply_buf.dtype)
        if s:
            last[s].start()
    enter_buf[pos] = reply_buf[pos]

    lax.fori_loop(cut2, wide_blocks, conv, 0)

    for k in range(1, reach + 1):
        @pl.when(zone + k < block_count)
        def _(k=k):
            onward(k).wait_send()
    q_load.wait()
    for copy in last.values():
        copy.wait()

    def finish(b, _):
        cols = pl.ds(pl.multiple_of(b * LANES, LANES), LANES)
        state = enter_buf[b // per_slice, :, pl.ds(pl.multiple_of((b % per_slice) * LANES, LANES), LANES)].astype(f32)
        spread = jnp.where(diagonal, jnp.concatenate([state] * (LANES // modes), axis=0), 0.0).astype(bf16)
        cross = jnp.dot(cross_table[:, cols], spread, preferred_element_type=f32)
        smoothed = (inner[:, cols] + cross).astype(bf16)
        out_buf[:, cols] = q_buf[:, cols] * smoothed
        return 0

    lax.fori_loop(0, lane_blocks, finish, 0, unroll=4)


def shards(query_gate, key_gate, values, rate_mix, residue, skip_gain, doc_lengths):
    ctx_count = lax.axis_size("ctx")
    head_count = lax.axis_size("head")
    devices = ctx_count * head_count
    tok, chans = query_gate.shape
    groups, modes = rate_mix.shape
    group_width = chans // groups
    total_tokens = tok * devices
    longest = total_tokens // 4
    block = min(devices // 4, chans // (4 * LANES))
    reach = -(-longest // (tok * block))
    width = chans // block
    wire = bf16
    vmem = pl.BlockSpec(memory_space=pltpu.VMEM)
    hbm = pl.BlockSpec(memory_space=pltpu.HBM)
    dma = pltpu.SemaphoreType.DMA
    whole = pltpu.VMEM((tok, chans), bf16)
    slices = pltpu.VMEM((block, modes, width), wire)
    def pin(x):
        return pltpu.with_memory_space_constraint(x, pltpu.HBM)

    return pl.pallas_call(
        functools.partial(kernel, (ctx_count, head_count, block, reach)),
        out_shape=jax.ShapeDtypeStruct((tok, chans), bf16),
        in_specs=[pl.BlockSpec(memory_space=pltpu.SMEM), hbm, hbm, hbm, vmem, vmem, vmem],
        out_specs=vmem,
        scratch_shapes=[
            whole, whole, whole, whole, pltpu.VMEM((tok, chans), f32), whole,
            pltpu.VMEM((modes, chans), f32), pltpu.VMEM((modes, chans), f32),
            pltpu.VMEM((1, chans), f32), pltpu.VMEM((1, chans), f32),
            slices, slices,
            pltpu.VMEM((block, modes, width), f32), pltpu.VMEM((block, modes, width), f32),
            slices, slices,
            pltpu.VMEM((modes, width), wire),
            pltpu.VMEM((reach, modes, width), wire),
            dma((2, block)), dma,
            dma((block - 1,)), dma((block - 1,)),
            dma((reach,)), dma((reach,)), dma((block - 1,)), dma((block - 1,)),
        ],
        compiler_params=pltpu.CompilerParams(collective_id=0, has_side_effects=True,
                                             vmem_limit_bytes=32 * 1024 * 1024),
    )(pin(doc_lengths), pin(query_gate), pin(key_gate), pin(values),
      pin(rate_mix.T), pin(residue.T), pin(skip_gain.reshape(1, -1)))


def solution(mesh):
    spans = P(("ctx", "head"), None)
    return jax.shard_map(
        shards,
        mesh=mesh,
        in_specs=(spans, spans, spans, P(), P(), P(), P()),
        out_specs=spans,
        check_vma=False,
    )
```

```python
import functools
import math

import jax
import jax.numpy as jnp
from jax import lax
from jax.experimental import pallas as pl
from jax.experimental.pallas import tpu as pltpu
from jax.sharding import PartitionSpec as P

LANES = 128
EARLY = 3
CUTS = (4, 6)
MESH = pl.DeviceIdType.MESH
f32 = jnp.float32
bf16 = jnp.bfloat16


def doc_start(tokens, ends):
    start = jnp.zeros_like(tokens)
    for end in ends:
        start = jnp.maximum(start, jnp.where(tokens >= end, end, 0))
    return start


def split_three(x):
    high = x.astype(bf16)
    rest = x - high.astype(f32)
    middle = rest.astype(bf16)
    low = (rest - middle.astype(f32)).astype(bf16)
    return [high, middle, low]


def kernel(cfg, lengths_hbm, q_hbm, k_hbm, v_hbm, rate_hbm, residue_hbm, skip_hbm,
           out_buf, q_buf, k_buf, v_buf, mixed, inner, cross_table,
           chan_rate, chan_weight, rate_row, weight_row,
           state_buf, gather_buf, prefix_buf, factor_buf, reply_buf, enter_buf, exit_buf, far_buf,
           lengths, rate_mix, residue, skip, small_sem, load_sem, q_sem, send1, recv1, send2, recv2, send3, recv3):
    ctx_count, head_count, block, reach = cfg
    devices = ctx_count * head_count
    tok, chans = mixed.shape
    modes = chan_rate.shape[0]
    lane_blocks = chans // LANES
    per_slice = lane_blocks // block
    group_width = LANES * modes // LANES
    block_count = devices // block
    me = lax.axis_index("ctx") * head_count + lax.axis_index("head")
    zone, pos = me // block, me % block
    span = me * tok

    def where_is(index):
        return (index // head_count, index % head_count)

    width = chans // block

    small = [pltpu.make_async_copy(src, dst, small_sem.at[n]) for n, (src, dst) in enumerate(
        ((rate_hbm, rate_mix), (residue_hbm, residue), (lengths_hbm, lengths), (skip_hbm, skip)))]
    for copy in small:
        copy.start()

    def mate_of(s):
        mate, bit = 0, 1
        while bit < block:
            mine = (pos // bit) % 2
            mate = mate + (1 - mine if s & bit else mine) * bit
            bit *= 2
        return mate

    order = sorted(range(block), key=lambda s: (-(s & ~head_count).bit_count(), s == 0))
    mates = {s: mate_of(s) for s in order}
    loads = {}
    for s in order:
        cols = pl.ds(pl.multiple_of(mates[s] * width, width), width)
        loads[s] = [pltpu.make_async_copy(src.at[:, cols], dst.at[:, cols], load_sem.at[n, s])
                    for n, (src, dst) in enumerate(((k_hbm, k_buf), (v_hbm, v_buf)))]
        for load in loads[s]:
            load.start()
    q_load = pltpu.make_async_copy(q_hbm, q_buf, q_sem)
    q_load.start()

    barrier = pltpu.get_barrier_semaphore()
    for s in order:
        if s:
            pl.semaphore_signal(barrier, inc=1, device_id=where_is(zone * block + mates[s]), device_id_type=MESH)
    for k in range(1, reach + 1):
        @pl.when(zone + k < block_count)
        def _(k=k):
            pl.semaphore_signal(barrier, inc=1, device_id=where_is(me + k * block), device_id_type=MESH)

        @pl.when(zone >= k)
        def _(k=k):
            pl.semaphore_signal(barrier, inc=1, device_id=where_is(me - k * block), device_id_type=MESH)

    rows = lax.broadcasted_iota(jnp.int32, (tok, LANES), 0)
    gr = lax.broadcasted_iota(jnp.int32, (LANES, LANES), 0) // modes
    gc = lax.broadcasted_iota(jnp.int32, (LANES, LANES), 1) // group_width
    diagonal = gr == gc

    small[0].wait()
    small[1].wait()
    rate = jnp.exp(-math.log(30.0) - rate_mix[...] * math.log(float(devices * tok)))
    double = 2.0 * rate
    one_minus = jnp.where(double < 1e-2,
                          double * (1.0 - double * (0.5 - double * (1.0 / 6.0 - double / 24.0))),
                          1.0 - jnp.exp(-double))
    weight = residue[...] * jnp.sqrt(one_minus)
    stacked = jnp.concatenate([p.astype(f32) for p in split_three(rate) + split_three(weight)], axis=0).astype(bf16)
    spread_to = LANES * group_width
    onto = jnp.where(lax.broadcasted_iota(jnp.int32, (LANES, spread_to), 0)
                     == lax.broadcasted_iota(jnp.int32, (LANES, spread_to), 1) // group_width, 1.0, 0.0).astype(bf16)
    own = (lax.broadcasted_iota(jnp.int32, (modes, spread_to), 0)
           == lax.broadcasted_iota(jnp.int32, (modes, spread_to), 1) % modes)
    for n in range(rate.shape[1] // LANES):
        wide_table = jnp.dot(stacked[:, n * LANES:(n + 1) * LANES], onto, preferred_element_type=f32)
        parts = [wide_table[m * modes:(m + 1) * modes] for m in range(6)]
        cols = slice(n * spread_to, (n + 1) * spread_to)
        for m, (table, row) in enumerate(((chan_rate, rate_row), (chan_weight, weight_row))):
            value = parts[3 * m] + (parts[3 * m + 1] + parts[3 * m + 2])
            table[:, cols] = value
            row[:, cols] = jnp.sum(jnp.where(own, value, 0.0), axis=0, keepdims=True)

    small[2].wait()
    small[3].wait()
    ends, total = [], jnp.int32(0)
    for n in range(lengths.shape[0]):
        total = total + lengths[n]
        ends.append(total)

    def start_of(token):
        return doc_start(jnp.full((modes, LANES), token, jnp.int32), ends)

    tail_start = start_of(span + tok - 1)[:1] - span
    tail = rows >= tail_start
    left = (tok - 1 - rows).astype(f32)

    expected = block - 1
    for k in range(1, reach + 1):
        expected = expected + jnp.where(zone + k < block_count, 1, 0) + jnp.where(zone >= k, 1, 0)

    def local(s):
        for load in loads[s]:
            load.wait()
        for i in range(per_slice):
            cols = pl.ds(pl.multiple_of(mates[s] * width + i * LANES, LANES), LANES)
            x = k_buf[:, cols] * v_buf[:, cols]
            mixed[:, cols] = x
            rate = rate_row[:, cols]
            table = jnp.where(tail, jnp.exp(-rate * left), 0.0).astype(bf16)
            full = lax.dot_general(table, x, (((0,), (0,)), ((), ())), preferred_element_type=f32)
            full = jnp.where(diagonal, full, 0.0)
            state = jnp.sum(full.reshape(LANES // modes, modes, LANES), axis=0)
            state_buf[mates[s], :, i * LANES:(i + 1) * LANES] = state.astype(state_buf.dtype)

    first = {s: pltpu.make_async_remote_copy(
        src_ref=state_buf.at[mates[s]], dst_ref=gather_buf.at[pos],
        send_sem=send1.at[s - 1], recv_sem=recv1.at[s - 1],
        device_id=where_is(zone * block + mates[s]), device_id_type=MESH) for s in order if s}

    early = order[:EARLY]
    for s in early:
        local(s)
    pl.semaphore_wait(barrier, expected)
    for s in early:
        first[s].start()
    for s in order[EARLY:]:
        local(s)
        if s:
            first[s].start()
    gather_buf[pos] = state_buf[pos]

    row_tok = span + rows
    row_start = doc_start(row_tok, ends) - span
    lane_iota = lax.broadcasted_iota(jnp.int32, (tok, tok), 1)
    row_iota = lax.broadcasted_iota(jnp.int32, (tok, tok), 0)
    mask = jnp.where((lane_iota >= row_start[:, :1]) & (lane_iota <= row_iota), 1.0, 0.0).astype(bf16)
    linked = row_start < 0
    ahead = (rows + 1).astype(f32)

    wide = 2 * LANES
    wide_blocks = chans // wide
    eights = lax.broadcasted_iota(jnp.int32, (8, wide), 0).astype(f32)

    def conv(b, _):
        cols = pl.ds(pl.multiple_of(b * wide, wide), wide)
        x = mixed[:, cols].astype(f32)
        total = skip[:, cols] * x
        for r in range(modes):
            rate = chan_rate[r:r + 1, cols]
            up = jnp.exp(rate * eights)
            down = chan_weight[r:r + 1, cols] * jnp.exp(-rate * eights)
            up_step = jnp.broadcast_to(jnp.exp(8.0 * rate), up.shape)
            down_step = jnp.broadcast_to(jnp.exp(-8.0 * rate), up.shape)
            ups, downs = [], []
            for _p in range(tok // 8):
                ups.append(up)
                downs.append(down)
                up, down = up * up_step, down * down_step
            scaled = (x * jnp.concatenate(ups, axis=0)).astype(bf16)
            summed = jnp.dot(mask, scaled, preferred_element_type=f32)
            total = total + jnp.concatenate(downs, axis=0) * summed
        inner[:, cols] = total
        return 0

    def entering_table(b, _):
        cols = pl.ds(pl.multiple_of(b * LANES, LANES), LANES)
        rate = rate_row[:, cols]
        weight = weight_row[:, cols]
        cross_table[:, cols] = jnp.where(linked, weight * jnp.exp(-rate * ahead), 0.0).astype(bf16)
        return 0

    cut1, cut2 = wide_blocks * CUTS[0] // 16, wide_blocks * CUTS[1] // 16
    lax.fori_loop(0, cut1, conv, 0)
    lax.fori_loop(0, lane_blocks, entering_table, 0, unroll=4)

    slice_rate = chan_rate[:, pl.ds(pl.multiple_of(pos * width, width), width)]
    decay = jnp.exp(-slice_rate * float(tok))

    def repeat_lanes(row):
        return jnp.concatenate([row] * (width // LANES), axis=1)

    def keep_of(index):
        crossing = start_of(index * tok + tok - 1) < index * tok
        return repeat_lanes(jnp.where(crossing, 1.0, 0.0))

    keeps = [keep_of(zone * block + e) * decay for e in range(block)]
    last_start = start_of(jnp.maximum(zone * block * tok - 1, 0))

    for copy in first.values():
        copy.wait()
    carry = jnp.zeros(slice_rate.shape, f32)
    factor = jnp.ones(slice_rate.shape, f32)
    for e in range(block):
        prefix_buf[e] = carry
        factor_buf[e] = factor
        step = keeps[e]
        carry = step * carry + gather_buf[e].astype(f32)
        factor = step * factor
    exit_buf[...] = carry.astype(exit_buf.dtype)

    def onward(k):
        return pltpu.make_async_remote_copy(
            src_ref=exit_buf, dst_ref=far_buf.at[k - 1],
            send_sem=send2.at[k - 1], recv_sem=recv2.at[k - 1],
            device_id=where_is(me + k * block), device_id_type=MESH)

    for k in range(1, reach + 1):
        @pl.when(zone + k < block_count)
        def _(k=k):
            onward(k).start()

    lax.fori_loop(cut1, cut2, conv, 0)

    for k in range(1, reach + 1):
        @pl.when(zone >= k)
        def _(k=k):
            onward(k).wait_recv()

        @pl.when(zone < k)
        def _(k=k):
            far_buf[k - 1] = jnp.zeros(far_buf.shape[1:], far_buf.dtype)

    far = jnp.zeros(slice_rate.shape, f32)
    for k in range(1, reach + 1):
        same = (last_start < (zone - k + 1) * block * tok)
        flag = repeat_lanes(jnp.where(same, 1.0, 0.0))
        scale = flag * jnp.exp(-slice_rate * float(tok * block * (k - 1)))
        far = far + scale * far_buf[k - 1].astype(f32)
    last = {s: pltpu.make_async_remote_copy(
        src_ref=reply_buf.at[mates[s]], dst_ref=enter_buf.at[pos],
        send_sem=send3.at[s - 1], recv_sem=recv3.at[s - 1],
        device_id=where_is(zone * block + mates[s]), device_id_type=MESH) for s in order if s}
    for s in order:
        reply_buf[mates[s]] = (prefix_buf[mates[s]] + factor_buf[mates[s]] * far).astype(reply_buf.dtype)
        if s:
            last[s].start()
    enter_buf[pos] = reply_buf[pos]

    lax.fori_loop(cut2, wide_blocks, conv, 0)

    for k in range(1, reach + 1):
        @pl.when(zone + k < block_count)
        def _(k=k):
            onward(k).wait_send()
    q_load.wait()
    for copy in last.values():
        copy.wait()

    def finish(b, _):
        cols = pl.ds(pl.multiple_of(b * LANES, LANES), LANES)
        state = enter_buf[b // per_slice, :, pl.ds(pl.multiple_of((b % per_slice) * LANES, LANES), LANES)].astype(f32)
        spread = jnp.where(diagonal, jnp.concatenate([state] * (LANES // modes), axis=0), 0.0).astype(bf16)
        cross = jnp.dot(cross_table[:, cols], spread, preferred_element_type=f32)
        smoothed = (inner[:, cols] + cross).astype(bf16)
        out_buf[:, cols] = q_buf[:, cols] * smoothed
        return 0

    lax.fori_loop(0, lane_blocks, finish, 0, unroll=16)


def shards(query_gate, key_gate, values, rate_mix, residue, skip_gain, doc_lengths):
    ctx_count = lax.axis_size("ctx")
    head_count = lax.axis_size("head")
    devices = ctx_count * head_count
    tok, chans = query_gate.shape
    groups, modes = rate_mix.shape
    group_width = chans // groups
    total_tokens = tok * devices
    longest = total_tokens // 4
    block = min(devices // 4, chans // (4 * LANES))
    reach = -(-longest // (tok * block))
    width = chans // block
    wire = bf16
    vmem = pl.BlockSpec(memory_space=pltpu.VMEM)
    hbm = pl.BlockSpec(memory_space=pltpu.HBM)
    dma = pltpu.SemaphoreType.DMA
    whole = pltpu.VMEM((tok, chans), bf16)
    slices = pltpu.VMEM((block, modes, width), wire)
    def pin(x):
        return pltpu.with_memory_space_constraint(x, pltpu.HBM)

    return pl.pallas_call(
        functools.partial(kernel, (ctx_count, head_count, block, reach)),
        out_shape=jax.ShapeDtypeStruct((tok, chans), bf16),
        in_specs=[hbm] * 7,
        out_specs=vmem,
        scratch_shapes=[
            whole, whole, whole, whole, pltpu.VMEM((tok, chans), f32), whole,
            pltpu.VMEM((modes, chans), f32), pltpu.VMEM((modes, chans), f32),
            pltpu.VMEM((1, chans), f32), pltpu.VMEM((1, chans), f32),
            slices, slices,
            pltpu.VMEM((block, modes, width), f32), pltpu.VMEM((block, modes, width), f32),
            slices, slices,
            pltpu.VMEM((modes, width), wire),
            pltpu.VMEM((reach, modes, width), wire),
            pltpu.SMEM(doc_lengths.shape, jnp.int32), pltpu.VMEM((modes, groups), f32),
            pltpu.VMEM((modes, groups), f32), pltpu.VMEM((1, chans), f32), dma((4,)),
            dma((2, block)), dma,
            dma((block - 1,)), dma((block - 1,)),
            dma((reach,)), dma((reach,)), dma((block - 1,)), dma((block - 1,)),
        ],
        compiler_params=pltpu.CompilerParams(collective_id=0, has_side_effects=True,
                                             vmem_limit_bytes=32 * 1024 * 1024),
    )(pin(doc_lengths), pin(query_gate), pin(key_gate), pin(values),
      pin(rate_mix.T), pin(residue.T), pin(skip_gain.reshape(1, -1)))


def solution(mesh):
    spans = P(("ctx", "head"), None)
    return jax.shard_map(
        shards,
        mesh=mesh,
        in_specs=(spans, spans, spans, P(), P(), P(), P()),
        out_specs=spans,
        check_vma=False,
    )
```
